1024 devices in a mesh: space: 64 (over x, z_lo, core), var: 16 (over y, z_hi).
Axes of the slice: x: 4, y: 8, z: 16 (z_hi: 2, z_lo: 8; z = z_hi * 8 + z_lo), core: 2. Of those that a mesh axis runs over, the one named last changes fastest.
Arguments:
- var_tokens: bfloat16 [64, 8192, 1024], P('var', 'space'), may hold values from -6 to 6
- key_query: bfloat16 [1024, 16], replicated
- value_weight: bfloat16 [1024, 1024], replicated, may hold values from -0.1875 to 0.1875
- qkv_weight: bfloat16 [1024, 3, 1024], P(None, None, 'var')
- out_weight: bfloat16 [1024, 1024], P('var'), may hold values from -0.1875 to 0.1875
- up_weight: bfloat16 [1024, 4096], P(None, 'var'), may hold values from -0.1875 to 0.1875
- down_weight: bfloat16 [4096, 1024], P('var'), may hold values from -0.09375 to 0.09375
- norm_gain: bfloat16 [1024], replicated, may hold values from 0.25 to 1.75
Outputs:
- block_out: bfloat16 [8192, 1024], P(('space', 'var'))
The draws below stay inside these ranges and needn't reach their ends.
All inputs are finite; a program needn't handle non-finite values.
Results may differ from the reference program's by a relative error of at most 0.018.
Values may be sent and summed in bfloat16 or wider, within the bound.
A program may use at most 32 MiB of HBM per device.

```python
import math
import jax
import jax.numpy as jnp
from jax import lax

D = 1024
H = 16
FF = 4096
HD = 64
VARS = 64
TOKENS = 8192


def draw_key_query(key, part):
    base = jax.random.normal(key, (D, H), jnp.float32) * (2.0 / math.sqrt(D))
    return base.astype(jnp.bfloat16)


def draw_qkv_weight(key, part):
    inv_root = 1.0 / math.sqrt(D)
    base_key = jax.random.fold_in(key, 11)
    widen = jnp.array([1.6, 1.6, 1.0], jnp.float32)
    result = jnp.clip(jax.random.normal(base_key, (D, 3, D), jnp.float32), -4.0, 4.0) * inv_root
    result = result * widen[None, :, None]
    return result.astype(jnp.bfloat16)


def steps_of(stream_key, dims, shards, low, high):
    def one(axis_at, parts):
        draws = jax.random.uniform(jax.random.fold_in(jax.random.fold_in(stream_key, 6), axis_at), (parts,), jnp.float32, low / len(shards), high / len(shards))
        return jnp.repeat(jnp.exp(draws), dims[axis_at] // parts).reshape((-1,) + (1,) * (len(dims) - axis_at - 1))

    loudness = one(*shards[0])
    for cut in shards[1:]:
        loudness = loudness * one(*cut)
    return loudness


def centred(own_key, extent, deviation, bound, split=(), kind=jnp.bfloat16):
    values = deviation * jax.random.normal(own_key, extent, jnp.float32)
    if split:
        values = values * steps_of(own_key, extent, split, -0.22, 0.18)
    return jnp.clip(values, -bound, bound).astype(kind)


def setup_inputs(seed: int = 0) -> dict:
    seeds = jax.random.split(jax.random.key(seed), 9)
    var_tokens = centred(seeds[0], (VARS, TOKENS, D), 1.0, 6.0, ((0, 16), (1, 64)))
    key_query = draw_key_query(jax.random.fold_in(seeds[8], 71), 0)
    value_weight = centred(seeds[2], (D, D), D ** -0.5, 0.1875)
    qkv_weight = draw_qkv_weight(jax.random.fold_in(seeds[8], 71), 0)
    out_weight = centred(seeds[4], (D, D), D ** -0.5, 0.1875, ((0, 16),))
    up_weight = centred(seeds[5], (D, FF), D ** -0.5, 0.1875, ((1, 16),))
    down_weight = centred(seeds[6], (FF, D), FF ** -0.5, 0.09375, ((0, 16),))
    norm_gain = jnp.clip(1.0 + 0.15 * jax.random.normal(seeds[7], (D,), jnp.float32), 0.25, 1.75).astype(jnp.bfloat16)
    return dict(var_tokens=var_tokens, key_query=key_query, value_weight=value_weight, qkv_weight=qkv_weight, out_weight=out_weight, up_weight=up_weight, down_weight=down_weight, norm_gain=norm_gain)


def reference(var_tokens, key_query, value_weight, qkv_weight, out_weight, up_weight, down_weight, norm_gain):
    f32 = jnp.float32
    bf16 = jnp.bfloat16
    block_len = math.gcd(512, TOKENS)
    block_count = TOKENS // block_len

    def pool_block(block_index):
        first_row = (block_index * block_len).astype(jnp.int32)
        tokens_blk = lax.dynamic_slice_in_dim(var_tokens, first_row, block_len, 1).astype(f32)
        scores = jnp.einsum('vsd,dh->vsh', tokens_blk, key_query.astype(f32))
        values = jnp.einsum('vsd,de->vse', tokens_blk, value_weight.astype(f32)).astype(bf16)
        values = values.reshape(VARS, block_len, H, HD)
        top_score = lax.optimization_barrier(jnp.max(scores, axis=0))
        exp_terms = jnp.exp(scores - top_score[None])
        weight_sum = lax.optimization_barrier(jnp.sum(exp_terms, axis=0))
        numerator = jnp.einsum('vsh,vshe->she', exp_terms.astype(bf16).astype(f32), values.astype(f32))
        return (numerator / weight_sum[..., None]).reshape(block_len, D).astype(bf16)
    pooled = lax.map(pool_block, jnp.arange(block_count, dtype=jnp.int32)).reshape(TOKENS, D)
    pooled_f = pooled.astype(f32)
    mean_row = lax.optimization_barrier(jnp.mean(pooled_f, axis=1, keepdims=True))
    centered = pooled_f - mean_row
    spread = lax.optimization_barrier(jnp.mean(centered * centered, axis=1, keepdims=True))
    normed = (centered * lax.rsqrt(spread + 1e-05) * norm_gain.astype(f32)).astype(bf16)
    qkv = jnp.einsum('td,dcj->tcj', normed.astype(f32), qkv_weight.astype(f32)).astype(bf16)
    query_all = qkv[:, 0].reshape(TOKENS, H, HD).transpose(1, 0, 2)
    key_all = qkv[:, 1].reshape(TOKENS, H, HD).transpose(1, 0, 2)
    value_all = qkv[:, 2].reshape(TOKENS, H, HD).transpose(1, 0, 2)

    def one_head(operands):
        query_h, key_h, value_h = operands
        logits = jnp.dot(query_h, key_h.T, preferred_element_type=f32) * HD ** (-0.5)
        top_logit = lax.optimization_barrier(jnp.max(logits, axis=1, keepdims=True))
        exp_terms = jnp.exp(logits - top_logit)
        att_total = lax.optimization_barrier(jnp.sum(exp_terms, axis=1, keepdims=True))
        summed = jnp.dot(exp_terms.astype(bf16), value_h, preferred_element_type=f32)
        return (summed / att_total).astype(bf16)
    attended = lax.map(one_head, (query_all, key_all, value_all))
    attended = attended.transpose(1, 0, 2).reshape(TOKENS, D)
    hidden = jax.nn.gelu(jnp.dot(normed, up_weight, preferred_element_type=f32), approximate=True).astype(bf16)
    total_out = pooled_f + jnp.dot(attended, out_weight, preferred_element_type=f32) + jnp.dot(hidden, down_weight, preferred_element_type=f32)
    return total_out.astype(bf16)
```

```python
import functools

import jax
import jax.numpy as jnp
from jax import lax
from jax.experimental import pallas as pl
from jax.experimental.pallas import tpu as pltpu
from jax.sharding import PartitionSpec as P

MESH = pl.DeviceIdType.MESH
F32 = jnp.float32
BF16 = jnp.bfloat16
HEAD = 64
NZH = 2
NZ = 8
NCORE = 2


def _dot(a, b, dims=(((1,), (0,)), ((), ()))):
    return lax.dot_general(a, b, dims, preferred_element_type=F32)


def _expander(heads, width):
    row = lax.broadcasted_iota(jnp.int32, (heads, width), 0)
    col = lax.broadcasted_iota(jnp.int32, (heads, width), 1)
    return jnp.where(col // HEAD == row, 1.0, 0.0).astype(BF16)


def _merge(outs, lses, spread):
    top = functools.reduce(jnp.maximum, lses)
    weights = [jnp.exp(lse - top) for lse in lses]
    total = functools.reduce(jnp.add, weights)
    shares = [w / total for w in weights]
    high = [s.astype(BF16) for s in shares]
    low = [(s - h.astype(F32)).astype(BF16) for s, h in zip(shares, high)]
    wide = _dot(jnp.concatenate(high + low, axis=0), spread)
    n, rows = len(outs), outs[0].shape[0]
    merged = None
    for k, out in enumerate(outs):
        share = wide[k * rows : (k + 1) * rows] + wide[(n + k) * rows : (n + k + 1) * rows]
        term = share * out.astype(F32)
        merged = term if merged is None else merged + term
    return merged, top + jnp.log(total)


def kernel(
    ny, ni, n_vars,
    tok_hbm, kq_ref, vw_hbm, qkv_hbm, ow_hbm, up_hbm, dw_hbm, gain_ref,
    out_ref,
    tok, vw, qkvw, ow, up, dw,
    part, stat, rpart, rstat, zpart, zstat, pooled, nbuf, kvbuf, qbuf, mlp,
    obuf, ostat, robuf, rostat, fbuf, rf, zsum, zrecv,
    load_sem, a_send, a_recv, as_send, as_recv, z_send, z_recv, n_send, n_recv,
    k_send, k_recv, q_send, q_recv, o_send, o_recv, os_send, os_recv, f_send, f_recv,
):
    rows = tok.shape[0] // n_vars
    width = tok.shape[1]
    heads = width // HEAD
    band = rows // ny

    space = lax.axis_index("space")
    var = lax.axis_index("var")
    y, zh = var // NZH, lax.rem(var, NZH)
    z = lax.rem(space // NCORE, NZ)
    i = (space // (NCORE * NZ)) * NCORE + lax.rem(space, NCORE)

    def at_y(d):
        return {"space": space, "var": lax.rem(y + d + ny, ny) * NZH + zh}

    def at_zh():
        return {"space": space, "var": y * NZH + (1 - zh)}

    def at_z(d):
        other = lax.rem(z + d, NZ)
        return {
            "space": (i // NCORE) * (NCORE * NZ) + other * NCORE + lax.rem(i, NCORE),
            "var": var,
        }

    def at_i(d):
        other = lax.rem(i + d + ni, ni)
        return {
            "space": (other // NCORE) * (NCORE * NZ) + z * NCORE + lax.rem(other, NCORE),
            "var": var,
        }

    def remote(src, dst, send, recv, peer):
        return pltpu.make_async_remote_copy(
            src_ref=src, dst_ref=dst, send_sem=send, recv_sem=recv,
            device_id=peer, device_id_type=MESH,
        )

    def far_first(n):
        return sorted(range(1, n), key=lambda d: -min(d, n - d))

    loads = [
        pltpu.make_async_copy(src, dst, load_sem.at[k])
        for k, (src, dst) in enumerate(
            [(tok_hbm, tok), (vw_hbm, vw), (qkv_hbm, qkvw), (up_hbm, up), (dw_hbm, dw), (ow_hbm, ow)]
        )
    ]
    for load in loads:
        load.start()

    barrier = pltpu.get_barrier_semaphore()
    greeted = 0
    for peers in (
        [at_y(d) for d in range(1, ny)], [at_zh()],
        [at_z(d) for d in range(1, NZ)], [at_i(d) for d in range(1, ni)],
    ):
        for peer in peers:
            pl.semaphore_signal(barrier, inc=1, device_id=peer, device_id_type=MESH)
            greeted += 1

    spread = _expander(heads, width)
    stat[...] = jnp.zeros_like(stat)
    zstat[0] = jnp.zeros_like(zstat[0])
    loads[0].wait()
    scores = _dot(tok[...], kq_ref[...])
    per_var = [scores[v * rows : (v + 1) * rows] for v in range(n_vars)]
    top = functools.reduce(jnp.maximum, per_var)
    exps = [jnp.exp(s - top) for s in per_var]
    total = functools.reduce(jnp.add, exps)
    stat[:, :heads] = top + jnp.log(total)
    shares = jnp.concatenate([(e / total).astype(BF16) for e in exps], axis=0)
    loads[1].wait()
    tile = min(256, width)
    for c in range(0, width, tile):
        values = _dot(tok[...], vw[:, c : c + tile]).astype(BF16).astype(F32)
        weighted = values * _dot(shares, spread[:, c : c + tile])
        acc = weighted[:rows]
        for v in range(1, n_vars):
            acc = acc + weighted[v * rows : (v + 1) * rows]
        part[:, c : c + tile] = acc.astype(BF16)

    pl.semaphore_wait(barrier, greeted)

    copies = []
    for d in far_first(ny):
        theirs = pl.ds(pl.multiple_of(lax.rem(y + d, ny) * band, band), band)
        for src, dst, send, recv in (
            (part, rpart, a_send, a_recv), (stat, rstat, as_send, as_recv)
        ):
            copy = remote(src.at[theirs], dst.at[d], send.at[d], recv.at[d], at_y(d))
            copy.start()
            copies.append(copy)
    for copy in copies:
        copy.wait()
    mine = pl.ds(pl.multiple_of(y * band, band), band)
    merged, lse = _merge(
        [part[mine, :]] + [rpart[d] for d in range(1, ny)],
        [stat[mine, :][:, :heads]] + [rstat[d][:, :heads] for d in range(1, ny)],
        spread,
    )

    zpart[0] = merged.astype(BF16)
    zstat[0, :, :heads] = lse
    copies = [
        remote(buf.at[0], buf.at[1], z_send.at[k], z_recv.at[k], at_zh())
        for k, buf in enumerate((zpart, zstat))
    ]
    for copy in copies:
        copy.start()
    for copy in copies:
        copy.wait()
    merged, _ = _merge(
        [zpart[0], zpart[1]], [zstat[0][:, :heads], zstat[1][:, :heads]], spread
    )
    rounded = merged.astype(BF16).astype(F32)
    pooled[...] = rounded
    centred = rounded - jnp.mean(rounded, axis=1, keepdims=True)
    spread_sq = jnp.mean(centred * centred, axis=1, keepdims=True)
    nbuf[0] = (centred * lax.rsqrt(spread_sq + 1e-05) * gain_ref[...].astype(F32)).astype(BF16)

    copies = []
    for d in far_first(ny):
        copy = remote(nbuf.at[0], nbuf.at[d], n_send.at[d], n_recv.at[d], at_y(d))
        copy.start()
        copies.append(copy)
    for copy in copies:
        copy.wait()
    normed = nbuf[...].reshape(rows, width)

    for load in loads[2:]:
        load.wait()
    qkv = _dot(normed, qkvw[...])
    kvbuf[0] = qkv[:, : 2 * HEAD].astype(BF16)
    qbuf[0] = (qkv[:, 2 * HEAD :] * HEAD**-0.5).astype(BF16)
    copies = []
    for d in range(NZ - 1, 0, -1):
        copy = remote(kvbuf.at[0], kvbuf.at[d], k_send.at[d], k_recv.at[d], at_z(d))
        copy.start()
        copies.append(copy)
    for d in far_first(ni):
        copy = remote(qbuf.at[0], qbuf.at[d], q_send.at[d], q_recv.at[d], at_i(d))
        copy.start()
        copies.append(copy)

    hidden = jax.nn.gelu(_dot(normed, up[...]), approximate=True).astype(BF16)
    mlp[...] = _dot(hidden, dw[...])
    for copy in copies:
        copy.wait()

    keys = NZ * rows
    kv = kvbuf[...].reshape(keys, 2 * HEAD)
    values_t = kv.T[HEAD:]

    def attend(d):
        logits = _dot(kv, qbuf[d], (((1,), (1,)), ((), ())))
        top = jnp.max(logits, axis=0, keepdims=True)
        exps = jnp.exp(logits - top)
        total = jnp.sum(exps, axis=0, keepdims=True)
        obuf[d] = (_dot(values_t, exps.astype(BF16)) / total).astype(BF16)
        ostat[d] = jnp.broadcast_to(top + jnp.log(total), (8, rows))

    def give(d):
        owner = at_i(-d)
        return (
            remote(obuf.at[d], robuf.at[d], o_send.at[d], o_recv.at[d], owner),
            remote(ostat.at[d], rostat.at[d], os_send.at[d], os_recv.at[d], owner),
        )

    @pl.loop(1, ni)
    def _(d):
        attend(d)
        for copy in give(d):
            copy.start()

    attend(0)
    for d in range(1, ni):
        for copy in give(d):
            copy.wait()
    lses = [ostat[0][:1]] + [rostat[d][:1] for d in range(1, ni)]
    top = functools.reduce(jnp.maximum, lses)
    weights = [jnp.exp(lse - top) for lse in lses]
    total = functools.reduce(jnp.add, weights)
    attended = obuf[0].astype(F32) * (weights[0] / total)
    for d in range(1, ni):
        attended = attended + robuf[d].astype(F32) * (weights[d] / total)

    term = _dot(attended.T.astype(BF16), ow[...]) + mlp[...]
    fbuf[...] = term.reshape(ny, band, width).astype(BF16)
    copies = []
    for d in far_first(ny):
        copy = remote(fbuf.at[d], rf.at[d], f_send.at[d], f_recv.at[d], at_y(-d))
        copy.start()
        copies.append(copy)
    for copy in copies:
        copy.wait()
    summed = term[:band]
    for d in range(1, ny):
        summed = summed + rf[d].astype(F32)
    zsum[...] = summed
    half = band // NZH
    own = pl.ds(pl.multiple_of(zh * half, half), half)
    other = pl.ds(pl.multiple_of((1 - zh) * half, half), half)
    last = remote(zsum.at[other], zrecv, z_send.at[2], z_recv.at[2], at_zh())
    last.start()
    last.wait()
    out_ref[...] = (pooled[own, :] + (zsum[own, :] + zrecv[...])).astype(BF16)


def per_device(var_tokens, key_query, value_weight, qkv_weight, out_weight, up_weight, down_weight, norm_gain):
    n_vars, rows, width = var_tokens.shape
    ny = lax.axis_size("var") // NZH
    ni = lax.axis_size("space") // NZ
    band = rows // ny
    hidden = up_weight.shape[1]
    blank = jnp.zeros((width, HEAD), BF16)
    qkv_cols = jnp.concatenate(
        [qkv_weight[:, 1], qkv_weight[:, 2], qkv_weight[:, 0], blank], axis=1
    )
    any_spec = pl.BlockSpec(memory_space=pl.ANY)
    vmem_spec = pl.BlockSpec(memory_space=pltpu.VMEM)
    dma = pltpu.SemaphoreType.DMA
    vm = pltpu.VMEM
    return pl.pallas_call(
        functools.partial(kernel, ny, ni, n_vars),
        out_shape=jax.ShapeDtypeStruct((band // NZH, width), BF16),
        in_specs=[any_spec, vmem_spec, any_spec, any_spec, any_spec, any_spec, any_spec, vmem_spec],
        out_specs=vmem_spec,
        scratch_shapes=[
            vm((n_vars * rows, width), BF16), vm((width, width), BF16), vm((width, 4 * HEAD), BF16),
            vm((HEAD, width), BF16), vm((width, hidden), BF16), vm((hidden, width), BF16),
            vm((rows, width), BF16), vm((rows, 128), F32),
            vm((ny, band, width), BF16), vm((ny, band, 128), F32),
            vm((2, band, width), BF16), vm((2, band, 128), F32),
            vm((band, width), F32), vm((ny, band, width), BF16),
            vm((NZ, rows, 2 * HEAD), BF16), vm((ni, rows, 2 * HEAD), BF16),
            vm((rows, width), F32),
            vm((ni, HEAD, rows), BF16), vm((ni, 8, rows), F32),
            vm((ni, HEAD, rows), BF16), vm((ni, 8, rows), F32),
            vm((ny, band, width), BF16), vm((ny, band, width), BF16),
            vm((band, width), F32), vm((band // NZH, width), F32),
            dma((6,)), dma((ny,)), dma((ny,)), dma((ny,)), dma((ny,)), dma((3,)), dma((3,)),
            dma((ny,)), dma((ny,)), dma((NZ,)), dma((NZ,)), dma((ni,)), dma((ni,)),
            dma((ni,)), dma((ni,)), dma((ni,)), dma((ni,)), dma((ny,)), dma((ny,)),
        ],
        compiler_params=pltpu.CompilerParams(collective_id=0, has_side_effects=True),
    )(
        var_tokens.reshape(n_vars * rows, width), key_query, value_weight, qkv_cols,
        out_weight, up_weight, down_weight, norm_gain.reshape(1, width),
    )


def solution(mesh):
    placed = (
        P("var", "space", None), P(), P(), P(None, None, "var"),
        P("var", None), P(None, "var"), P("var", None), P(),
    )
    return jax.shard_map(
        per_device, mesh=mesh, in_specs=placed, out_specs=P(("space", "var"), None), check_vma=False
    )
```

```python
import functools

import jax
import jax.numpy as jnp
from jax import lax
from jax.experimental import pallas as pl
from jax.experimental.pallas import tpu as pltpu
from jax.sharding import PartitionSpec as P

MESH = pl.DeviceIdType.MESH
F32 = jnp.float32
BF16 = jnp.bfloat16
HEAD = 64
NZH = 2
NZ = 8
NCORE = 2
CHUNKS = 2
TRANSPOSED = (((1,), (1,)), ((), ()))


def _dot(a, b, dims=(((1,), (0,)), ((), ()))):
    return lax.dot_general(a, b, dims, preferred_element_type=F32)


def _expander(heads, width):
    row = lax.broadcasted_iota(jnp.int32, (heads, width), 0)
    col = lax.broadcasted_iota(jnp.int32, (heads, width), 1)
    return jnp.where(col // HEAD == row, 1.0, 0.0).astype(BF16)


def _shares(lses):
    top = functools.reduce(jnp.maximum, lses)
    weights = [jnp.exp(lse - top) for lse in lses]
    total = functools.reduce(jnp.add, weights)
    return [w / total for w in weights], top + jnp.log(total)


def _widen(shares, spread):
    high = [s.astype(BF16) for s in shares]
    low = [(s - h.astype(F32)).astype(BF16) for s, h in zip(shares, high)]
    wide = _dot(jnp.concatenate(high + low, axis=0), spread)
    half = wide.shape[0] // 2
    return wide[:half] + wide[half:]


def _weigh(outs, wide):
    rows = outs[0].shape[0]
    terms = [wide[k * rows : (k + 1) * rows] * out.astype(F32) for k, out in enumerate(outs)]
    return functools.reduce(jnp.add, terms)


def kernel(
    ny, ni, n_vars,
    tok_hbm, kq_hbm, vw_hbm, qkv_hbm, ow_hbm, up_hbm, dw_hbm, gain_ref,
    out_ref,
    tok, kq, vw, qkvw, ow, up, dw,
    part, stat, rpart, rstat, zpart, zstat, pooled, nbuf, kvbuf, qbuf, mlp,
    near_out, near_stat, obuf, ostat, robuf, rostat, fbuf, rf, zsum, zsend, zrecv,
    load_sem, a_send, a_recv, as_send, as_recv, z_send, z_recv, n_send, n_recv,
    k_send, k_recv, q_send, q_recv, o_send, o_recv, os_send, os_recv, f_send, f_recv,
):
    rows = tok.shape[0] // n_vars
    width = tok.shape[1]
    heads = width // HEAD
    band = rows // ny
    cols = width // CHUNKS

    space = lax.axis_index("space")
    var = lax.axis_index("var")
    y, zh = var // NZH, lax.rem(var, NZH)
    z = lax.rem(space // NCORE, NZ)
    i = (space // (NCORE * NZ)) * NCORE + lax.rem(space, NCORE)

    def at_y(d):
        return {"space": space, "var": lax.rem(y + d + ny, ny) * NZH + zh}

    def at_zh():
        return {"space": space, "var": y * NZH + (1 - zh)}

    def at_z(t):
        other, bit = 0, 1
        while bit < NZ:
            mine = lax.rem(z // bit, 2)
            other = other + bit * ((1 - mine) if t & bit else mine)
            bit *= 2
        return {
            "space": (i // NCORE) * (NCORE * NZ) + other * NCORE + lax.rem(i, NCORE),
            "var": var,
        }

    def at_i(d):
        other = lax.rem(i + d + ni, ni)
        return {
            "space": (other // NCORE) * (NCORE * NZ) + z * NCORE + lax.rem(other, NCORE),
            "var": var,
        }

    started = []

    def remote(src, dst, send, recv, peer):
        return pltpu.make_async_remote_copy(
            src_ref=src, dst_ref=dst, send_sem=send, recv_sem=recv,
            device_id=peer, device_id_type=MESH,
        )

    def go(*args):
        copy = remote(*args)
        copy.start()
        started.append(copy)
        return copy

    def far_first(n):
        return sorted(range(1, n), key=lambda d: -min(d, n - d))

    moves = [(tok_hbm, tok), (kq_hbm, kq)]
    moves += [(vw_hbm.at[:, c * cols : (c + 1) * cols], vw.at[c]) for c in range(CHUNKS)]
    moves += [
        (qkv_hbm.at[:HEAD], qkvw.at[2 * HEAD : 3 * HEAD]),
        (qkv_hbm.at[HEAD:], qkvw.at[: 2 * HEAD]),
        (up_hbm, up), (dw_hbm, dw), (ow_hbm, ow),
    ]
    loads = [pltpu.make_async_copy(src, dst, load_sem.at[k]) for k, (src, dst) in enumerate(moves)]
    barrier = pltpu.get_barrier_semaphore()
    greeted = 0
    for peers in (
        [at_zh()], [at_z(t) for t in range(1, NZ)],
        [at_y(d) for d in range(1, ny)], [at_i(d) for d in range(1, ni)],
    ):
        for peer in peers:
            pl.semaphore_signal(barrier, inc=1, device_id=peer, device_id_type=MESH)
            greeted += 1
    for load in loads:
        load.start()

    spread = _expander(heads, width)
    stat[...] = jnp.zeros_like(stat)
    zstat[0] = jnp.zeros_like(zstat[0])
    loads[0].wait()
    loads[1].wait()
    scores = _dot(tok[...], kq[...], TRANSPOSED)
    per_var = [scores[v * rows : (v + 1) * rows] for v in range(n_vars)]
    top = functools.reduce(jnp.maximum, per_var)
    exps = [jnp.exp(s - top) for s in per_var]
    total = functools.reduce(jnp.add, exps)
    stat[:, :heads] = top + jnp.log(total)
    shares = jnp.concatenate([(e / total).astype(BF16) for e in exps], axis=0)

    a_copies, stat_copies = [], []
    tile = min(256, cols)
    for c in range(CHUNKS):
        loads[2 + c].wait()
        for k in range(0, cols, tile):
            values = _dot(tok[...], vw[c, :, k : k + tile]).astype(BF16).astype(F32)
            weighted = values * _dot(shares, spread[:, c * cols + k : c * cols + k + tile])
            acc = weighted[:rows]
            for v in range(1, n_vars):
                acc = acc + weighted[v * rows : (v + 1) * rows]
            part[c, :, k : k + tile] = acc.astype(BF16)
        if c == 0:
            pl.semaphore_wait(barrier, greeted)
        a_copies.append([])
        for d in far_first(ny):
            theirs = pl.ds(pl.multiple_of(lax.rem(y + d, ny) * band, band), band)
            if c == 0:
                stat_copies.append(
                    go(stat.at[theirs], rstat.at[d], as_send.at[d], as_recv.at[d], at_y(d))
                )
            a_copies[c].append(
                go(part.at[c, theirs], rpart.at[c, d], a_send.at[c, d], a_recv.at[c, d], at_y(d))
            )

    mine = pl.ds(pl.multiple_of(y * band, band), band)
    for copy in stat_copies:
        copy.wait_recv()
    shares, lse = _shares(
        [stat[mine, :][:, :heads]] + [rstat[d][:, :heads] for d in range(1, ny)]
    )
    zstat[0, :, :heads] = lse
    stat_copy = go(zstat.at[0], zstat.at[1], z_send.at[0], z_recv.at[0], at_zh())
    wide = _widen(shares, spread)
    z_copies = []
    for c in range(CHUNKS):
        for copy in a_copies[c]:
            copy.wait_recv()
        zpart[c, 0] = _weigh(
            [part[c, mine, :]] + [rpart[c, d] for d in range(1, ny)],
            wide[:, c * cols : (c + 1) * cols],
        ).astype(BF16)
        z_copies.append(
            go(zpart.at[c, 0], zpart.at[c, 1], z_send.at[1 + c], z_recv.at[1 + c], at_zh())
        )
    stat_copy.wait_recv()
    shares, _ = _shares([zstat[0][:, :heads], zstat[1][:, :heads]])
    wide = _widen(shares, spread)
    for c in range(CHUNKS):
        z_copies[c].wait_recv()
        cut = slice(c * cols, (c + 1) * cols)
        merged = _weigh([zpart[c, 0], zpart[c, 1]], wide[:, cut])
        pooled[:, cut] = merged.astype(BF16).astype(F32)
    rounded = pooled[...]
    centred = rounded - jnp.mean(rounded, axis=1, keepdims=True)
    spread_sq = jnp.mean(centred * centred, axis=1, keepdims=True)
    gain = gain_ref[...].astype(F32).reshape(1, width)
    nbuf[0] = (centred * lax.rsqrt(spread_sq + 1e-05) * gain).astype(BF16)

    copies = [
        go(nbuf.at[0], nbuf.at[d], n_send.at[d], n_recv.at[d], at_y(d)) for d in far_first(ny)
    ]
    qkvw[3 * HEAD :] = jnp.zeros_like(qkvw[3 * HEAD :])
    for load in loads[2 + CHUNKS :]:
        load.wait()
    for copy in copies:
        copy.wait_recv()
    normed = nbuf[...].reshape(rows, width)

    qkv = _dot(normed, qkvw[...], TRANSPOSED)
    kvbuf[0] = qkv[:, : 2 * HEAD].astype(BF16)
    qbuf[0] = (qkv[:, 2 * HEAD :] * HEAD**-0.5).astype(BF16)
    k_copies = {
        t: go(kvbuf.at[0], kvbuf.at[t], k_send.at[t], k_recv.at[t], at_z(t))
        for t in range(NZ - 1, 0, -1)
    }
    q_copies = [
        go(qbuf.at[0], qbuf.at[d], q_send.at[d], q_recv.at[d], at_i(d)) for d in far_first(ni)
    ]
    hidden = jax.nn.gelu(_dot(normed, up[...]), approximate=True).astype(BF16)
    mlp[...] = _dot(hidden, dw[...])

    keys = NZ // 2 * rows

    def logits_of(kv, p):
        return _dot(kv, qbuf[pl.ds(2 * p, 2)].reshape(2 * rows, 2 * HEAD), TRANSPOSED)

    for copy in q_copies:
        copy.wait_recv()
    for t in range(1, NZ // 2):
        k_copies[t].wait_recv()
    near = kvbuf[: NZ // 2].reshape(keys, 2 * HEAD)
    near_values = near.T[HEAD:]

    @pl.loop(0, ni // 2)
    def _(p):
        logits = logits_of(near, p)
        top = jnp.max(logits, axis=0, keepdims=True)
        exps = jnp.exp(logits - top)
        total = jnp.sum(exps, axis=0, keepdims=True)
        near_out[p] = _dot(near_values, exps.astype(BF16))
        near_stat[p, :8] = jnp.broadcast_to(top, (8, 2 * rows))
        near_stat[p, 8:] = jnp.broadcast_to(total, (8, 2 * rows))

    for t in range(NZ // 2, NZ):
        k_copies[t].wait_recv()
    far = kvbuf[NZ // 2 :].reshape(keys, 2 * HEAD)
    far_values = far.T[HEAD:]

    def finish(p):
        logits = logits_of(far, p)
        near_top = near_stat[p, :1]
        top = jnp.maximum(near_top, jnp.max(logits, axis=0, keepdims=True))
        exps = jnp.exp(logits - top)
        scale = jnp.exp(near_top - top)
        total = jnp.sum(exps, axis=0, keepdims=True) + scale * near_stat[p, 8:9]
        out = (_dot(far_values, exps.astype(BF16)) + scale * near_out[p]) / total
        lse = jnp.broadcast_to(top + jnp.log(total), (8, 2 * rows))
        for k in range(2):
            obuf[2 * p + k] = out[:, k * rows : (k + 1) * rows].astype(BF16)
            ostat[2 * p + k] = lse[:, k * rows : (k + 1) * rows]

    def give(d):
        owner = at_i(-d)
        return (
            remote(obuf.at[d], robuf.at[d], o_send.at[d], o_recv.at[d], owner),
            remote(ostat.at[d], rostat.at[d], os_send.at[d], os_recv.at[d], owner),
        )

    @pl.loop(1, ni // 2)
    def _(p):
        finish(p)
        for k in range(2):
            for copy in give(2 * p + k):
                copy.start()

    finish(0)
    for copy in give(1):
        copy.start()
    for d in range(1, ni):
        for copy in give(d):
            started.append(copy)
            copy.wait_recv()
    shares, _ = _shares([ostat[0][:1]] + [rostat[d][:1] for d in range(1, ni)])
    attended = obuf[0].astype(F32) * shares[0]
    for d in range(1, ni):
        attended = attended + robuf[d].astype(F32) * shares[d]

    attended = attended.T.astype(BF16)
    f_copies = []
    for c in range(CHUNKS):
        cut = slice(c * cols, (c + 1) * cols)
        term = _dot(attended, ow[:, cut]) + mlp[:, cut]
        zsum[:, cut] = term[:band]
        fbuf[c] = term.reshape(ny, band, cols).astype(BF16)
        f_copies.append([
            go(fbuf.at[c, d], rf.at[c, d], f_send.at[c, d], f_recv.at[c, d], at_y(-d))
            for d in far_first(ny)
        ])
    half = band // NZH
    own = pl.ds(pl.multiple_of(zh * half, half), half)
    other = pl.ds(pl.multiple_of((1 - zh) * half, half), half)
    z_copies = []
    for c in range(CHUNKS):
        cut = slice(c * cols, (c + 1) * cols)
        for copy in f_copies[c]:
            copy.wait_recv()
        summed = zsum[:, cut]
        for d in range(1, ny):
            summed = summed + rf[c, d].astype(F32)
        zsum[:, cut] = summed
        zsend[c] = zsum[other, cut].astype(BF16)
        sem = 1 + CHUNKS + c
        z_copies.append(go(zsend.at[c], zrecv.at[c], z_send.at[sem], z_recv.at[sem], at_zh()))
    for c in range(CHUNKS):
        cut = slice(c * cols, (c + 1) * cols)
        z_copies[c].wait_recv()
        out_ref[:, cut] = (
            pooled[own, cut] + (zsum[own, cut] + zrecv[c].astype(F32))
        ).astype(BF16)
    for copy in started:
        copy.wait_send()


def per_device(var_tokens, key_query, value_weight, qkv_weight, out_weight, up_weight, down_weight, norm_gain):
    n_vars, rows, width = var_tokens.shape
    ny = lax.axis_size("var") // NZH
    ni = lax.axis_size("space") // NZ
    band = rows // ny
    hidden = up_weight.shape[1]
    cols = width // CHUNKS
    half = band // NZH
    any_spec = pl.BlockSpec(memory_space=pl.ANY)
    vmem_spec = pl.BlockSpec(memory_space=pltpu.VMEM)
    dma = pltpu.SemaphoreType.DMA
    vm = pltpu.VMEM
    return pl.pallas_call(
        functools.partial(kernel, ny, ni, n_vars),
        out_shape=jax.ShapeDtypeStruct((half, width), BF16),
        in_specs=[any_spec] * 7 + [vmem_spec],
        out_specs=vmem_spec,
        scratch_shapes=[
            vm((n_vars * rows, width), BF16), vm(key_query.shape[::-1], BF16), vm((CHUNKS, width, cols), BF16),
            vm((4 * HEAD, width), BF16), vm((HEAD, width), BF16), vm((width, hidden), BF16), vm((hidden, width), BF16),
            vm((CHUNKS, rows, cols), BF16), vm((rows, 128), F32),
            vm((CHUNKS, ny, band, cols), BF16), vm((ny, band, 128), F32),
            vm((CHUNKS, 2, band, cols), BF16), vm((2, band, 128), F32),
            vm((band, width), F32), vm((ny, band, width), BF16),
            vm((NZ, rows, 2 * HEAD), BF16), vm((ni, rows, 2 * HEAD), BF16),
            vm((rows, width), F32),
            vm((ni // 2, HEAD, 2 * rows), F32), vm((ni // 2, 16, 2 * rows), F32),
            vm((ni, HEAD, rows), BF16), vm((ni, 8, rows), F32),
            vm((ni, HEAD, rows), BF16), vm((ni, 8, rows), F32),
            vm((CHUNKS, ny, band, cols), BF16), vm((CHUNKS, ny, band, cols), BF16),
            vm((band, width), F32), vm((CHUNKS, half, cols), BF16), vm((CHUNKS, half, cols), BF16),
            dma((7 + CHUNKS,)), dma((CHUNKS, ny)), dma((CHUNKS, ny)), dma((ny,)), dma((ny,)),
            dma((1 + 2 * CHUNKS,)), dma((1 + 2 * CHUNKS,)),
            dma((ny,)), dma((ny,)), dma((NZ,)), dma((NZ,)), dma((ni,)), dma((ni,)),
            dma((ni,)), dma((ni,)), dma((ni,)), dma((ni,)), dma((CHUNKS, ny)), dma((CHUNKS, ny)),
        ],
        compiler_params=pltpu.CompilerParams(collective_id=0, has_side_effects=True),
    )(
        var_tokens.reshape(n_vars * rows, width), key_query.T, value_weight,
        qkv_weight.transpose(1, 2, 0).reshape(3 * HEAD, width),
        out_weight, up_weight, down_weight, norm_gain,
    )


def solution(mesh):
    placed = (
        P("var", "space", None), P(), P(), P(None, None, "var"),
        P("var", None), P(None, "var"), P("var", None), P(),
    )
    return jax.shard_map(
        per_device, mesh=mesh, in_specs=placed, out_specs=P(("space", "var"), None), check_vma=False
    )
```

```python
import functools

import jax
import jax.numpy as jnp
from jax import lax
from jax.experimental import pallas as pl
from jax.experimental.pallas import tpu as pltpu
from jax.sharding import PartitionSpec as P

MESH = pl.DeviceIdType.MESH
F32 = jnp.float32
BF16 = jnp.bfloat16
HEAD = 64
NZH = 2
NZ = 8
NCORE = 2
CHUNKS = 4
GROUP = 4
TRANSPOSED = (((1,), (1,)), ((), ()))


def _dot(a, b, dims=(((1,), (0,)), ((), ()))):
    return lax.dot_general(a, b, dims, preferred_element_type=F32)


def _expander(heads, width):
    row = lax.broadcasted_iota(jnp.int32, (heads, width), 0)
    col = lax.broadcasted_iota(jnp.int32, (heads, width), 1)
    return jnp.where(col // HEAD == row, 1.0, 0.0).astype(BF16)


def _shares(lses):
    top = functools.reduce(jnp.maximum, lses)
    weights = [jnp.exp(lse - top) for lse in lses]
    total = functools.reduce(jnp.add, weights)
    return [w / total for w in weights], top + jnp.log(total)


def _widen(shares, spread):
    high = [s.astype(BF16) for s in shares]
    low = [(s - h.astype(F32)).astype(BF16) for s, h in zip(shares, high)]
    wide = _dot(jnp.concatenate(high + low, axis=0), spread)
    half = wide.shape[0] // 2
    return wide[:half] + wide[half:]


def _pack(lse):
    *lead, rows, heads = lse.shape
    pair = lse.reshape(*lead, 2, rows // 2, heads)
    return jnp.concatenate([pair[..., 0, :, :], pair[..., 1, :, :]], axis=-1)


def _unpack(packed, heads):
    return jnp.concatenate([packed[:, :heads], packed[:, heads : 2 * heads]], axis=0)


def _weigh(outs, wide):
    rows = outs[0].shape[0]
    terms = [wide[k * rows : (k + 1) * rows] * out.astype(F32) for k, out in enumerate(outs)]
    return functools.reduce(jnp.add, terms)


def kernel(
    ny, ni, n_vars,
    tok_hbm, kq_hbm, vw_hbm, qkv_hbm, ow_hbm, up_hbm, dw_hbm, gain_ref,
    out_ref,
    tok, kq, vw, qkvw, ow, up, dw,
    part, stat, rpart, rstat, zpart, zstat, pooled, nbuf, kvbuf, qbuf, mlp,
    near_out, near_stat, obuf, ostat, robuf, rostat, fbuf, rf, zsum, zsend, zrecv,
    load_sem, a_send, a_recv, as_send, as_recv, z_send, z_recv, n_send, n_recv,
    k_send, k_recv, q_send, q_recv, o_send, o_recv, os_send, os_recv, f_send, f_recv,
):
    rows = tok.shape[0] // n_vars
    width = tok.shape[1]
    heads = width // HEAD
    band = rows // ny
    cols = width // CHUNKS

    space = lax.axis_index("space")
    var = lax.axis_index("var")
    y, zh = var // NZH, lax.rem(var, NZH)
    z = lax.rem(space // NCORE, NZ)
    i = (space // (NCORE * NZ)) * NCORE + lax.rem(space, NCORE)

    def at_y(d):
        return {"space": space, "var": lax.rem(y + d + ny, ny) * NZH + zh}

    def at_zh():
        return {"space": space, "var": y * NZH + (1 - zh)}

    def at_z(t):
        other, bit = 0, 1
        while bit < NZ:
            mine = lax.rem(z // bit, 2)
            other = other + bit * ((1 - mine) if t & bit else mine)
            bit *= 2
        return {
            "space": (i // NCORE) * (NCORE * NZ) + other * NCORE + lax.rem(i, NCORE),
            "var": var,
        }

    def at_i(d):
        other = lax.rem(i + d + ni, ni)
        return {
            "space": (other // NCORE) * (NCORE * NZ) + z * NCORE + lax.rem(other, NCORE),
            "var": var,
        }

    started = []

    def remote(src, dst, send, recv, peer):
        return pltpu.make_async_remote_copy(
            src_ref=src, dst_ref=dst, send_sem=send, recv_sem=recv,
            device_id=peer, device_id_type=MESH,
        )

    def go(*args):
        copy = remote(*args)
        copy.start()
        started.append(copy)
        return copy

    def far_first(n):
        return sorted(range(1, n), key=lambda d: -min(d, n - d))

    moves = [(tok_hbm, tok), (kq_hbm, kq)]
    moves += [(vw_hbm.at[:, c * cols : (c + 1) * cols], vw.at[c]) for c in range(CHUNKS)]
    moves += [
        (qkv_hbm.at[:HEAD], qkvw.at[2 * HEAD : 3 * HEAD]),
        (qkv_hbm.at[HEAD:], qkvw.at[: 2 * HEAD]),
        (up_hbm, up), (dw_hbm, dw), (ow_hbm, ow),
    ]
    loads = [pltpu.make_async_copy(src, dst, load_sem.at[k]) for k, (src, dst) in enumerate(moves)]
    barrier = pltpu.get_barrier_semaphore()
    greeted = 0
    for peers in (
        [at_zh()], [at_z(t) for t in range(1, NZ)],
        [at_y(d) for d in range(1, ny)], [at_i(d) for d in range(1, ni)],
    ):
        for peer in peers:
            pl.semaphore_signal(barrier, inc=1, device_id=peer, device_id_type=MESH)
            greeted += 1
    for load in loads:
        load.start()

    spread = _expander(heads, width)
    stat[...] = jnp.zeros_like(stat)
    zstat[0] = jnp.zeros_like(zstat[0])
    loads[0].wait()
    loads[1].wait()
    scores = _dot(tok[...], kq[...], TRANSPOSED)
    per_var = [scores[v * rows : (v + 1) * rows] for v in range(n_vars)]
    top = functools.reduce(jnp.maximum, per_var)
    exps = [jnp.exp(s - top) for s in per_var]
    total = functools.reduce(jnp.add, exps)
    stat[:, :, : 2 * heads] = _pack((top + jnp.log(total)).reshape(ny, band, heads))
    shares = jnp.concatenate([(e / total).astype(BF16) for e in exps], axis=0)

    a_copies, stat_copies = [], []
    tile = min(256, cols)
    for c in range(CHUNKS):
        loads[2 + c].wait()
        for k in range(0, cols, tile):
            values = _dot(tok[...], vw[c, :, k : k + tile]).astype(BF16).astype(F32)
            weighted = values * _dot(shares, spread[:, c * cols + k : c * cols + k + tile])
            acc = weighted[:rows]
            for v in range(1, n_vars):
                acc = acc + weighted[v * rows : (v + 1) * rows]
            part[c, :, k : k + tile] = acc.astype(BF16)
        if c == 0:
            pl.semaphore_wait(barrier, greeted)
        a_copies.append([])
        for d in far_first(ny):
            peer = lax.rem(y + d, ny)
            theirs = pl.ds(pl.multiple_of(peer * band, band), band)
            if c == 0:
                stat_copies.append(
                    go(stat.at[peer], rstat.at[d], as_send.at[d], as_recv.at[d], at_y(d))
                )
            a_copies[c].append(
                go(part.at[c, theirs], rpart.at[c, d], a_send.at[c, d], a_recv.at[c, d], at_y(d))
            )

    mine = pl.ds(pl.multiple_of(y * band, band), band)
    for copy in stat_copies:
        copy.wait_recv()
    shares, lse = _shares(
        [_unpack(stat[y], heads)] + [_unpack(rstat[d], heads) for d in range(1, ny)]
    )
    zstat[0, :, : 2 * heads] = _pack(lse)
    stat_copy = go(zstat.at[0], zstat.at[1], z_send.at[0], z_recv.at[0], at_zh())
    wide = _widen(shares, spread)
    z_copies = []
    for c in range(CHUNKS):
        for copy in a_copies[c]:
            copy.wait_recv()
        zpart[c, 0] = _weigh(
            [part[c, mine, :]] + [rpart[c, d] for d in range(1, ny)],
            wide[:, c * cols : (c + 1) * cols],
        ).astype(BF16)
        z_copies.append(
            go(zpart.at[c, 0], zpart.at[c, 1], z_send.at[1 + c], z_recv.at[1 + c], at_zh())
        )
    stat_copy.wait_recv()
    shares, _ = _shares([_unpack(zstat[k], heads) for k in range(2)])
    wide = _widen(shares, spread)
    for c in range(CHUNKS):
        z_copies[c].wait_recv()
        cut = slice(c * cols, (c + 1) * cols)
        merged = _weigh([zpart[c, 0], zpart[c, 1]], wide[:, cut])
        pooled[:, cut] = merged.astype(BF16).astype(F32)
    rounded = pooled[...]
    centred = rounded - jnp.mean(rounded, axis=1, keepdims=True)
    spread_sq = jnp.mean(centred * centred, axis=1, keepdims=True)
    gain = gain_ref[...].astype(F32).reshape(1, width)
    nbuf[0] = (centred * lax.rsqrt(spread_sq + 1e-05) * gain).astype(BF16)

    copies = [
        go(nbuf.at[0], nbuf.at[d], n_send.at[d], n_recv.at[d], at_y(d)) for d in far_first(ny)
    ]
    qkvw[3 * HEAD :] = jnp.zeros_like(qkvw[3 * HEAD :])
    for load in loads[2 + CHUNKS :]:
        load.wait()
    for copy in copies:
        copy.wait_recv()
    normed = nbuf[...].reshape(rows, width)

    qkv = _dot(normed, qkvw[...], TRANSPOSED)
    kvbuf[0] = qkv[:, : 2 * HEAD].astype(BF16)
    qbuf[0] = (qkv[:, 2 * HEAD :] * HEAD**-0.5).astype(BF16)
    k_copies = {
        t: go(kvbuf.at[0], kvbuf.at[t], k_send.at[t], k_recv.at[t], at_z(t))
        for t in range(NZ - 1, 0, -1)
    }
    q_copies = [
        go(qbuf.at[0], qbuf.at[d], q_send.at[d], q_recv.at[d], at_i(d)) for d in far_first(ni)
    ]
    hidden = jax.nn.gelu(_dot(normed, up[...]), approximate=True).astype(BF16)
    mlp[...] = _dot(hidden, dw[...])

    keys = NZ // 2 * rows
    group = min(GROUP, ni)
    wide_rows = group * rows
    order = range(ni // group - 1, -1, -1)

    def logits_of(kv, p):
        return _dot(kv, qbuf[p * group : (p + 1) * group].reshape(wide_rows, 2 * HEAD), TRANSPOSED)

    for copy in q_copies:
        copy.wait_recv()
    for t in range(1, NZ // 2):
        k_copies[t].wait_recv()
    near = kvbuf[: NZ // 2].reshape(keys, 2 * HEAD)
    near_values = near.T[HEAD:]

    for p in order:
        logits = logits_of(near, p)
        top = jnp.max(logits, axis=0, keepdims=True)
        exps = jnp.exp(logits - top)
        total = jnp.sum(exps, axis=0, keepdims=True)
        near_out[p] = _dot(near_values, exps.astype(BF16))
        near_stat[p, :8] = jnp.broadcast_to(top, (8, wide_rows))
        near_stat[p, 8:] = jnp.broadcast_to(total, (8, wide_rows))

    for t in range(NZ // 2, NZ):
        k_copies[t].wait_recv()
    far = kvbuf[NZ // 2 :].reshape(keys, 2 * HEAD)
    far_values = far.T[HEAD:]

    def finish(p):
        logits = logits_of(far, p)
        near_top = near_stat[p, :1]
        top = jnp.maximum(near_top, jnp.max(logits, axis=0, keepdims=True))
        exps = jnp.exp(logits - top)
        scale = jnp.exp(near_top - top)
        total = jnp.sum(exps, axis=0, keepdims=True) + scale * near_stat[p, 8:9]
        out = (_dot(far_values, exps.astype(BF16)) + scale * near_out[p]) / total
        lse = jnp.broadcast_to(top + jnp.log(total), (8, wide_rows))
        for k in range(group):
            obuf[group * p + k] = out[:, k * rows : (k + 1) * rows].astype(BF16)
            ostat[group * p + k] = lse[:, k * rows : (k + 1) * rows]

    returns = []
    for p in order:
        finish(p)
        for d in range(max(1, p * group), (p + 1) * group):
            owner = at_i(-d)
            returns.append(go(obuf.at[d], robuf.at[d], o_send.at[d], o_recv.at[d], owner))
            returns.append(go(ostat.at[d], rostat.at[d], os_send.at[d], os_recv.at[d], owner))
    for copy in returns:
        copy.wait_recv()
    shares, _ = _shares([ostat[0][:1]] + [rostat[d][:1] for d in range(1, ni)])
    attended = obuf[0].astype(F32) * shares[0]
    for d in range(1, ni):
        attended = attended + robuf[d].astype(F32) * shares[d]

    term = _dot(attended.T.astype(BF16), ow[...]) + mlp[...]
    half = band // NZH
    bands = term.reshape(ny, NZH, half, width)
    for h in range(NZH):
        fbuf[h] = bands[:, h].astype(BF16)
        zsum[h] = bands[0, h]
    f_copies = []
    for stage, h in enumerate((1 - zh, zh)):
        f_copies.append([
            go(fbuf.at[h, d], rf.at[stage, d], f_send.at[stage, d], f_recv.at[stage, d], at_y(-d))
            for d in far_first(ny)
        ])

    def summed(stage, h):
        for copy in f_copies[stage]:
            copy.wait_recv()
        total = zsum[h]
        for d in range(1, ny):
            total = total + rf[stage, d].astype(F32)
        return total

    zsend[...] = summed(0, 1 - zh).astype(BF16)
    last = go(zsend, zrecv, z_send.at[1 + CHUNKS], z_recv.at[1 + CHUNKS], at_zh())
    own = pl.ds(pl.multiple_of(zh * half, half), half)
    mine = summed(1, zh) + pooled[own, :]
    last.wait_recv()
    out_ref[...] = (mine + zrecv[...].astype(F32)).astype(BF16)
    for copy in started:
        copy.wait_send()


def per_device(var_tokens, key_query, value_weight, qkv_weight, out_weight, up_weight, down_weight, norm_gain):
    n_vars, rows, width = var_tokens.shape
    ny = lax.axis_size("var") // NZH
    ni = lax.axis_size("space") // NZ
    band = rows // ny
    hidden = up_weight.shape[1]
    cols = width // CHUNKS
    half = band // NZH
    group = min(GROUP, ni)
    any_spec = pl.BlockSpec(memory_space=pl.ANY)
    vmem_spec = pl.BlockSpec(memory_space=pltpu.VMEM)
    dma = pltpu.SemaphoreType.DMA
    vm = pltpu.VMEM
    return pl.pallas_call(
        functools.partial(kernel, ny, ni, n_vars),
        out_shape=jax.ShapeDtypeStruct((half, width), BF16),
        in_specs=[any_spec] * 7 + [vmem_spec],
        out_specs=vmem_spec,
        scratch_shapes=[
            vm((n_vars * rows, width), BF16), vm(key_query.shape[::-1], BF16), vm((CHUNKS, width, cols), BF16),
            vm((4 * HEAD, width), BF16), vm((HEAD, width), BF16), vm((width, hidden), BF16), vm((hidden, width), BF16),
            vm((CHUNKS, rows, cols), BF16), vm((ny, band // 2, 128), F32),
            vm((CHUNKS, ny, band, cols), BF16), vm((ny, band // 2, 128), F32),
            vm((CHUNKS, 2, band, cols), BF16), vm((2, band // 2, 128), F32),
            vm((band, width), F32), vm((ny, band, width), BF16),
            vm((NZ, rows, 2 * HEAD), BF16), vm((ni, rows, 2 * HEAD), BF16),
            vm((rows, width), F32),
            vm((ni // group, HEAD, group * rows), F32), vm((ni // group, 16, group * rows), F32),
            vm((ni, HEAD, rows), BF16), vm((ni, 8, rows), F32),
            vm((ni, HEAD, rows), BF16), vm((ni, 8, rows), F32),
            vm((NZH, ny, half, width), BF16), vm((NZH, ny, half, width), BF16),
            vm((NZH, half, width), F32), vm((half, width), BF16), vm((half, width), BF16),
            dma((7 + CHUNKS,)), dma((CHUNKS, ny)), dma((CHUNKS, ny)), dma((ny,)), dma((ny,)),
            dma((2 + CHUNKS,)), dma((2 + CHUNKS,)),
            dma((ny,)), dma((ny,)), dma((NZ,)), dma((NZ,)), dma((ni,)), dma((ni,)),
            dma((ni,)), dma((ni,)), dma((ni,)), dma((ni,)), dma((NZH, ny)), dma((NZH, ny)),
        ],
        compiler_params=pltpu.CompilerParams(collective_id=0, has_side_effects=True),
    )(
        var_tokens.reshape(n_vars * rows, width), key_query.T, value_weight,
        qkv_weight.transpose(1, 2, 0).reshape(3 * HEAD, width),
        out_weight, up_weight, down_weight, norm_gain,
    )


def solution(mesh):
    placed = (
        P("var", "space", None), P(), P(), P(None, None, "var"),
        P("var", None), P(None, "var"), P("var", None), P(),
    )
    return jax.shard_map(
        per_device, mesh=mesh, in_specs=placed, out_specs=P(("space", "var"), None), check_vma=False
    )
```

```python
import functools

import jax
import jax.numpy as jnp
from jax import lax
from jax.experimental import pallas as pl
from jax.experimental.pallas import tpu as pltpu
from jax.sharding import PartitionSpec as P

MESH = pl.DeviceIdType.MESH
F32 = jnp.float32
BF16 = jnp.bfloat16
HEAD = 64
NZH = 2
NZ = 8
NCORE = 2
CHUNKS = 4
GROUP = 4
TRANSPOSED = (((1,), (1,)), ((), ()))


def _dot(a, b, dims=(((1,), (0,)), ((), ()))):
    return lax.dot_general(a, b, dims, preferred_element_type=F32)


def _expander(heads, width):
    row = lax.broadcasted_iota(jnp.int32, (heads, width), 0)
    col = lax.broadcasted_iota(jnp.int32, (heads, width), 1)
    return jnp.where(col // HEAD == row, 1.0, 0.0).astype(BF16)


def _shares(lses):
    top = functools.reduce(jnp.maximum, lses)
    weights = [jnp.exp(lse - top) for lse in lses]
    total = functools.reduce(jnp.add, weights)
    return [w / total for w in weights], top + jnp.log(total)


def _widen(shares, spread):
    high = [s.astype(BF16) for s in shares]
    low = [(s - h.astype(F32)).astype(BF16) for s, h in zip(shares, high)]
    wide = _dot(jnp.concatenate(high + low, axis=0), spread)
    half = wide.shape[0] // 2
    return wide[:half] + wide[half:]


def _pack(lse):
    *lead, rows, heads = lse.shape
    pair = lse.reshape(*lead, 2, rows // 2, heads)
    return jnp.concatenate([pair[..., 0, :, :], pair[..., 1, :, :]], axis=-1)


def _unpack(packed, heads):
    return jnp.concatenate([packed[:, :heads], packed[:, heads : 2 * heads]], axis=0)


def _weigh(outs, wide):
    rows = outs[0].shape[0]
    terms = [wide[k * rows : (k + 1) * rows] * out.astype(F32) for k, out in enumerate(outs)]
    return functools.reduce(jnp.add, terms)


def kernel(
    ny, ni, n_vars,
    tok_hbm, kq_hbm, vw_hbm, qkv_hbm, ow_hbm, up_hbm, dw_hbm, gain_ref,
    out_ref,
    tok, kq, vw, qkvw, ow, up, dw,
    part, stat, rpart, rstat, zpart, zstat, pooled, nbuf, kvbuf, qbuf, mlp,
    near_out, near_stat, obuf, ostat, robuf, rostat, fbuf, rf, zsum, zsend, zrecv,
    load_sem, a_send, a_recv, as_send, as_recv, z_send, z_recv, n_send, n_recv,
    k_send, k_recv, q_send, q_recv, o_send, o_recv, os_send, os_recv, f_send, f_recv,
):
    rows = tok.shape[0] // n_vars
    width = tok.shape[1]
    heads = width // HEAD
    band = rows // ny
    cols = width // CHUNKS

    space = lax.axis_index("space")
    var = lax.axis_index("var")
    y, zh = var // NZH, lax.rem(var, NZH)
    z = lax.rem(space // NCORE, NZ)
    i = (space // (NCORE * NZ)) * NCORE + lax.rem(space, NCORE)

    def at_y(d):
        return {"space": space, "var": lax.rem(y + d + ny, ny) * NZH + zh}

    def at_zh():
        return {"space": space, "var": y * NZH + (1 - zh)}

    def at_z(t):
        other, bit = 0, 1
        while bit < NZ:
            mine = lax.rem(z // bit, 2)
            other = other + bit * ((1 - mine) if t & bit else mine)
            bit *= 2
        return {
            "space": (i // NCORE) * (NCORE * NZ) + other * NCORE + lax.rem(i, NCORE),
            "var": var,
        }

    def at_i(d):
        other = lax.rem(i + d + ni, ni)
        return {
            "space": (other // NCORE) * (NCORE * NZ) + z * NCORE + lax.rem(other, NCORE),
            "var": var,
        }

    started = []

    def remote(src, dst, send, recv, peer):
        return pltpu.make_async_remote_copy(
            src_ref=src, dst_ref=dst, send_sem=send, recv_sem=recv,
            device_id=peer, device_id_type=MESH,
        )

    def go(*args):
        copy = remote(*args)
        copy.start()
        started.append(copy)
        return copy

    def far_first(n):
        return sorted(range(1, n), key=lambda d: -min(d, n - d))

    moves = [(tok_hbm, tok), (kq_hbm, kq)]
    moves += [(vw_hbm.at[:, c * cols : (c + 1) * cols], vw.at[c]) for c in range(CHUNKS)]
    moves += [
        (qkv_hbm.at[:HEAD], qkvw.at[2 * HEAD : 3 * HEAD]),
        (qkv_hbm.at[HEAD:], qkvw.at[: 2 * HEAD]),
        (up_hbm, up), (dw_hbm, dw), (ow_hbm, ow),
    ]
    loads = [pltpu.make_async_copy(src, dst, load_sem.at[k]) for k, (src, dst) in enumerate(moves)]
    barrier = pltpu.get_barrier_semaphore()
    greeted = 0
    for peers in (
        [at_zh()], [at_z(t) for t in range(1, NZ)],
        [at_y(d) for d in range(1, ny)], [at_i(d) for d in range(1, ni)],
    ):
        for peer in peers:
            pl.semaphore_signal(barrier, inc=1, device_id=peer, device_id_type=MESH)
            greeted += 1
    for load in loads:
        load.start()

    spread = _expander(heads, width)
    stat[...] = jnp.zeros_like(stat)
    zstat[0] = jnp.zeros_like(zstat[0])
    loads[0].wait()
    loads[1].wait()
    scores = _dot(tok[...], kq[...], TRANSPOSED)
    per_var = [scores[v * rows : (v + 1) * rows] for v in range(n_vars)]
    top = functools.reduce(jnp.maximum, per_var)
    exps = [jnp.exp(s - top) for s in per_var]
    total = functools.reduce(jnp.add, exps)
    stat[:, :, : 2 * heads] = _pack((top + jnp.log(total)).reshape(ny, band, heads))
    shares = jnp.concatenate([(e / total).astype(BF16) for e in exps], axis=0)

    a_copies, stat_copies = [], []
    tile = min(256, cols)
    for c in range(CHUNKS):
        loads[2 + c].wait()
        for k in range(0, cols, tile):
            values = _dot(tok[...], vw[c, :, k : k + tile]).astype(BF16).astype(F32)
            weighted = values * _dot(shares, spread[:, c * cols + k : c * cols + k + tile])
            acc = weighted[:rows]
            for v in range(1, n_vars):
                acc = acc + weighted[v * rows : (v + 1) * rows]
            part[c, :, k : k + tile] = acc.astype(BF16)
        if c == 0:
            pl.semaphore_wait(barrier, greeted)
        a_copies.append([])
        for d in far_first(ny):
            peer = lax.rem(y + d, ny)
            theirs = pl.ds(pl.multiple_of(peer * band, band), band)
            if c == 0:
                stat_copies.append(
                    go(stat.at[peer], rstat.at[d], as_send.at[d], as_recv.at[d], at_y(d))
                )
            a_copies[c].append(
                go(part.at[c, theirs], rpart.at[c, d], a_send.at[c, d], a_recv.at[c, d], at_y(d))
            )

    mine = pl.ds(pl.multiple_of(y * band, band), band)
    for copy in stat_copies:
        copy.wait_recv()
    shares, lse = _shares(
        [_unpack(stat[y], heads)] + [_unpack(rstat[d], heads) for d in range(1, ny)]
    )
    zstat[0, :, : 2 * heads] = _pack(lse)
    stat_copy = go(zstat.at[0], zstat.at[1], z_send.at[0], z_recv.at[0], at_zh())
    wide = _widen(shares, spread)
    z_copies = []
    for c in range(CHUNKS):
        for copy in a_copies[c]:
            copy.wait_recv()
        zpart[c, 0] = _weigh(
            [part[c, mine, :]] + [rpart[c, d] for d in range(1, ny)],
            wide[:, c * cols : (c + 1) * cols],
        ).astype(BF16)
        z_copies.append(
            go(zpart.at[c, 0], zpart.at[c, 1], z_send.at[1 + c], z_recv.at[1 + c], at_zh())
        )
    stat_copy.wait_recv()
    shares, _ = _shares([_unpack(zstat[k], heads) for k in range(2)])
    wide = _widen(shares, spread)
    for c in range(CHUNKS):
        z_copies[c].wait_recv()
        cut = slice(c * cols, (c + 1) * cols)
        merged = _weigh([zpart[c, 0], zpart[c, 1]], wide[:, cut])
        pooled[:, cut] = merged.astype(BF16).astype(F32)
    rounded = pooled[...]
    centred = rounded - jnp.mean(rounded, axis=1, keepdims=True)
    spread_sq = jnp.mean(centred * centred, axis=1, keepdims=True)
    gain = gain_ref[...].astype(F32).reshape(1, width)
    nbuf[0] = (centred * lax.rsqrt(spread_sq + 1e-05) * gain).astype(BF16)

    n_copies = {
        d: go(nbuf.at[0], nbuf.at[d], n_send.at[d], n_recv.at[d], at_y(d))
        for d in [*range(ny // 2 - 1, 0, -1), *range(ny // 2, ny)]
    }
    qkvw[3 * HEAD :] = jnp.zeros_like(qkvw[3 * HEAD :])
    for load in loads[2 + CHUNKS : 4 + CHUNKS]:
        load.wait()

    k_copies = {t: [] for t in range(1, NZ)}
    for h in range(2):
        bands = range(h * ny // 2, (h + 1) * ny // 2)
        for d in bands:
            if d:
                n_copies[d].wait_recv()
        some = nbuf[bands.start : bands.stop].reshape(rows // 2, width)
        qkv = _dot(some, qkvw[...], TRANSPOSED)
        cut = slice(h * rows // 2, (h + 1) * rows // 2)
        kvbuf[0, cut] = qkv[:, : 2 * HEAD].astype(BF16)
        qbuf[0, cut] = (qkv[:, 2 * HEAD :] * HEAD**-0.5).astype(BF16)
        for t in range(NZ - 1, 0, -1):
            k_copies[t].append(
                go(kvbuf.at[0, cut], kvbuf.at[t, cut], k_send.at[h, t], k_recv.at[h, t], at_z(t))
            )
    q_copies = [
        go(qbuf.at[0], qbuf.at[d], q_send.at[d], q_recv.at[d], at_i(d)) for d in far_first(ni)
    ]
    for load in loads[4 + CHUNKS :]:
        load.wait()
    normed = nbuf[...].reshape(rows, width)
    hidden = jax.nn.gelu(_dot(normed, up[...]), approximate=True).astype(BF16)
    mlp[...] = _dot(hidden, dw[...])

    keys = NZ // 2 * rows
    group = min(GROUP, ni)
    wide_rows = group * rows
    order = range(ni // group - 1, -1, -1)

    def logits_of(kv, p):
        return _dot(kv, qbuf[p * group : (p + 1) * group].reshape(wide_rows, 2 * HEAD), TRANSPOSED)

    for copy in q_copies:
        copy.wait_recv()
    for t in range(1, NZ // 2):
        for copy in k_copies[t]:
            copy.wait_recv()
    near = kvbuf[: NZ // 2].reshape(keys, 2 * HEAD)
    near_values = near.T[HEAD:]

    for p in order:
        logits = logits_of(near, p)
        top = jnp.max(logits, axis=0, keepdims=True)
        exps = jnp.exp(logits - top)
        total = jnp.sum(exps, axis=0, keepdims=True)
        near_out[p] = _dot(near_values, exps.astype(BF16))
        near_stat[p, :8] = jnp.broadcast_to(top, (8, wide_rows))
        near_stat[p, 8:] = jnp.broadcast_to(total, (8, wide_rows))

    for t in range(NZ // 2, NZ):
        for copy in k_copies[t]:
            copy.wait_recv()
    far = kvbuf[NZ // 2 :].reshape(keys, 2 * HEAD)
    far_values = far.T[HEAD:]

    def finish(p):
        logits = logits_of(far, p)
        near_top = near_stat[p, :1]
        top = jnp.maximum(near_top, jnp.max(logits, axis=0, keepdims=True))
        exps = jnp.exp(logits - top)
        scale = jnp.exp(near_top - top)
        total = jnp.sum(exps, axis=0, keepdims=True) + scale * near_stat[p, 8:9]
        out = (_dot(far_values, exps.astype(BF16)) + scale * near_out[p]) / total
        lse = jnp.broadcast_to(top + jnp.log(total), (8, wide_rows))
        for k in range(group):
            obuf[group * p + k] = out[:, k * rows : (k + 1) * rows].astype(BF16)
            ostat[group * p + k] = lse[:, k * rows : (k + 1) * rows]

    returns = []
    for p in order:
        finish(p)
        for d in range(max(1, p * group), (p + 1) * group):
            owner = at_i(-d)
            returns.append(go(obuf.at[d], robuf.at[d], o_send.at[d], o_recv.at[d], owner))
            returns.append(go(ostat.at[d], rostat.at[d], os_send.at[d], os_recv.at[d], owner))
    for copy in returns:
        copy.wait_recv()
    shares, _ = _shares([ostat[0][:1]] + [rostat[d][:1] for d in range(1, ni)])
    attended = obuf[0].astype(F32) * shares[0]
    for d in range(1, ni):
        attended = attended + robuf[d].astype(F32) * shares[d]

    term = _dot(attended.T.astype(BF16), ow[...]) + mlp[...]
    half = band // NZH
    bands = term.reshape(ny, NZH, half, width)
    for h in range(NZH):
        fbuf[h] = bands[:, h].astype(BF16)
        zsum[h] = bands[0, h]
    f_copies = []
    for stage, h in enumerate((1 - zh, zh)):
        f_copies.append([
            go(fbuf.at[h, d], rf.at[stage, d], f_send.at[stage, d], f_recv.at[stage, d], at_y(-d))
            for d in far_first(ny)
        ])

    def summed(stage, h):
        for copy in f_copies[stage]:
            copy.wait_recv()
        total = zsum[h]
        for d in range(1, ny):
            total = total + rf[stage, d].astype(F32)
        return total

    zsend[...] = summed(0, 1 - zh).astype(BF16)
    last = go(zsend, zrecv, z_send.at[1 + CHUNKS], z_recv.at[1 + CHUNKS], at_zh())
    own = pl.ds(pl.multiple_of(zh * half, half), half)
    mine = summed(1, zh) + pooled[own, :]
    last.wait_recv()
    out_ref[...] = (mine + zrecv[...].astype(F32)).astype(BF16)
    for copy in started:
        copy.wait_send()


def per_device(var_tokens, key_query, value_weight, qkv_weight, out_weight, up_weight, down_weight, norm_gain):
    n_vars, rows, width = var_tokens.shape
    ny = lax.axis_size("var") // NZH
    ni = lax.axis_size("space") // NZ
    band = rows // ny
    hidden = up_weight.shape[1]
    cols = width // CHUNKS
    half = band // NZH
    group = min(GROUP, ni)
    any_spec = pl.BlockSpec(memory_space=pl.ANY)
    vmem_spec = pl.BlockSpec(memory_space=pltpu.VMEM)
    dma = pltpu.SemaphoreType.DMA
    vm = pltpu.VMEM
    return pl.pallas_call(
        functools.partial(kernel, ny, ni, n_vars),
        out_shape=jax.ShapeDtypeStruct((half, width), BF16),
        in_specs=[any_spec] * 7 + [vmem_spec],
        out_specs=vmem_spec,
        scratch_shapes=[
            vm((n_vars * rows, width), BF16), vm(key_query.shape[::-1], BF16), vm((CHUNKS, width, cols), BF16),
            vm((4 * HEAD, width), BF16), vm((HEAD, width), BF16), vm((width, hidden), BF16), vm((hidden, width), BF16),
            vm((CHUNKS, rows, cols), BF16), vm((ny, band // 2, 128), F32),
            vm((CHUNKS, ny, band, cols), BF16), vm((ny, band // 2, 128), F32),
            vm((CHUNKS, 2, band, cols), BF16), vm((2, band // 2, 128), F32),
            vm((band, width), F32), vm((ny, band, width), BF16),
            vm((NZ, rows, 2 * HEAD), BF16), vm((ni, rows, 2 * HEAD), BF16),
            vm((rows, width), F32),
            vm((ni // group, HEAD, group * rows), F32), vm((ni // group, 16, group * rows), F32),
            vm((ni, HEAD, rows), BF16), vm((ni, 8, rows), F32),
            vm((ni, HEAD, rows), BF16), vm((ni, 8, rows), F32),
            vm((NZH, ny, half, width), BF16), vm((NZH, ny, half, width), BF16),
            vm((NZH, half, width), F32), vm((half, width), BF16), vm((half, width), BF16),
            dma((7 + CHUNKS,)), dma((CHUNKS, ny)), dma((CHUNKS, ny)), dma((ny,)), dma((ny,)),
            dma((2 + CHUNKS,)), dma((2 + CHUNKS,)),
            dma((ny,)), dma((ny,)), dma((2, NZ)), dma((2, NZ)), dma((ni,)), dma((ni,)),
            dma((ni,)), dma((ni,)), dma((ni,)), dma((ni,)), dma((NZH, ny)), dma((NZH, ny)),
        ],
        compiler_params=pltpu.CompilerParams(collective_id=0, has_side_effects=True),
    )(
        var_tokens.reshape(n_vars * rows, width), key_query.T, value_weight,
        qkv_weight.transpose(1, 2, 0).reshape(3 * HEAD, width),
        out_weight, up_weight, down_weight, norm_gain,
    )


def solution(mesh):
    placed = (
        P("var", "space", None), P(), P(), P(None, None, "var"),
        P("var", None), P(None, "var"), P("var", None), P(),
    )
    return jax.shard_map(
        per_device, mesh=mesh, in_specs=placed, out_specs=P(("space", "var"), None), check_vma=False
    )
```

```python
import functools

import jax
import jax.numpy as jnp
from jax import lax
from jax.experimental import pallas as pl
from jax.experimental.pallas import tpu as pltpu
from jax.sharding import PartitionSpec as P

MESH = pl.DeviceIdType.MESH
F32 = jnp.float32
BF16 = jnp.bfloat16
HEAD = 64
NZH = 2
NZ = 8
NCORE = 2
CHUNKS = 4
GROUP = 4
TRANSPOSED = (((1,), (1,)), ((), ()))


def _dot(a, b, dims=(((1,), (0,)), ((), ()))):
    return lax.dot_general(a, b, dims, preferred_element_type=F32)


def _expander(heads, width):
    row = lax.broadcasted_iota(jnp.int32, (heads, width), 0)
    col = lax.broadcasted_iota(jnp.int32, (heads, width), 1)
    return jnp.where(col // HEAD == row, 1.0, 0.0).astype(BF16)


def _shares(lses):
    top = functools.reduce(jnp.maximum, lses)
    weights = [jnp.exp(lse - top) for lse in lses]
    total = functools.reduce(jnp.add, weights)
    return [w / total for w in weights], top + jnp.log(total)


def _widen(shares, spread):
    high = [s.astype(BF16) for s in shares]
    low = [(s - h.astype(F32)).astype(BF16) for s, h in zip(shares, high)]
    wide = _dot(jnp.concatenate(high + low, axis=0), spread)
    half = wide.shape[0] // 2
    return wide[:half] + wide[half:]


def _pack(lse):
    *lead, rows, heads = lse.shape
    pair = lse.reshape(*lead, 2, rows // 2, heads)
    return jnp.concatenate([pair[..., 0, :, :], pair[..., 1, :, :]], axis=-1)


def _unpack(packed, heads):
    return jnp.concatenate([packed[:, :heads], packed[:, heads : 2 * heads]], axis=0)


def _weigh(outs, wide):
    rows = outs[0].shape[0]
    terms = [wide[k * rows : (k + 1) * rows] * out.astype(F32) for k, out in enumerate(outs)]
    return functools.reduce(jnp.add, terms)


def kernel(
    ny, ni, n_vars,
    tok_hbm, kq_hbm, vw_hbm, qkv_hbm, ow_hbm, up_hbm, dw_hbm, gain_ref,
    out_ref,
    tok, kq, vw, qkvw, ow, up, dw,
    part, stat, rpart, rstat, zpart, zstat, pooled, nbuf, kvbuf, qbuf, mlp,
    run_out, run_stat, obuf, ostat, robuf, rostat, fbuf, rf, zsum, zsend, zrecv,
    load_sem, a_send, a_recv, as_send, as_recv, z_send, z_recv, n_send, n_recv,
    k_send, k_recv, q_send, q_recv, o_send, o_recv, os_send, os_recv, f_send, f_recv,
):
    rows = tok.shape[0] // n_vars
    width = tok.shape[1]
    heads = width // HEAD
    band = rows // ny
    cols = width // CHUNKS

    space = lax.axis_index("space")
    var = lax.axis_index("var")
    y, zh = var // NZH, lax.rem(var, NZH)
    z = lax.rem(space // NCORE, NZ)
    i = (space // (NCORE * NZ)) * NCORE + lax.rem(space, NCORE)

    def at_y(d):
        return {"space": space, "var": lax.rem(y + d + ny, ny) * NZH + zh}

    def at_zh():
        return {"space": space, "var": y * NZH + (1 - zh)}

    def at_z(t):
        other, bit = 0, 1
        while bit < NZ:
            mine = lax.rem(z // bit, 2)
            other = other + bit * ((1 - mine) if t & bit else mine)
            bit *= 2
        return {
            "space": (i // NCORE) * (NCORE * NZ) + other * NCORE + lax.rem(i, NCORE),
            "var": var,
        }

    def at_i(d):
        other = lax.rem(i + d + ni, ni)
        return {
            "space": (other // NCORE) * (NCORE * NZ) + z * NCORE + lax.rem(other, NCORE),
            "var": var,
        }

    started = []

    def remote(src, dst, send, recv, peer):
        return pltpu.make_async_remote_copy(
            src_ref=src, dst_ref=dst, send_sem=send, recv_sem=recv,
            device_id=peer, device_id_type=MESH,
        )

    def go(*args):
        copy = remote(*args)
        copy.start()
        started.append(copy)
        return copy

    def far_first(n):
        return sorted(range(1, n), key=lambda d: -min(d, n - d))

    moves = [(tok_hbm, tok), (kq_hbm, kq)]
    moves += [(vw_hbm.at[:, c * cols : (c + 1) * cols], vw.at[c]) for c in range(CHUNKS)]
    moves += [
        (qkv_hbm.at[:HEAD], qkvw.at[2 * HEAD : 3 * HEAD]),
        (qkv_hbm.at[HEAD:], qkvw.at[: 2 * HEAD]),
        (up_hbm, up), (dw_hbm, dw), (ow_hbm, ow),
    ]
    loads = [pltpu.make_async_copy(src, dst, load_sem.at[k]) for k, (src, dst) in enumerate(moves)]
    barrier = pltpu.get_barrier_semaphore()
    far_peers = [at_zh()] + [at_z(t) for t in range(1, NZ)]
    near_peers = [at_y(d) for d in range(1, ny)] + [at_i(d) for d in range(1, ni)]
    greeted = len(far_peers) + len(near_peers)
    for peer in far_peers:
        pl.semaphore_signal(barrier, inc=1, device_id=peer, device_id_type=MESH)
    for load in loads:
        load.start()
    for peer in near_peers:
        pl.semaphore_signal(barrier, inc=1, device_id=peer, device_id_type=MESH)

    spread = _expander(heads, width)
    stat[...] = jnp.zeros_like(stat)
    zstat[0] = jnp.zeros_like(zstat[0])
    loads[0].wait()
    loads[1].wait()
    scores = _dot(tok[...], kq[...], TRANSPOSED)
    per_var = [scores[v * rows : (v + 1) * rows] for v in range(n_vars)]
    top = functools.reduce(jnp.maximum, per_var)
    exps = [jnp.exp(s - top) for s in per_var]
    total = functools.reduce(jnp.add, exps)
    stat[:, :, : 2 * heads] = _pack((top + jnp.log(total)).reshape(ny, band, heads))
    shares = jnp.concatenate([(e / total).astype(BF16) for e in exps], axis=0)

    a_copies, stat_copies = [], []
    tile = min(256, cols)
    for c in range(CHUNKS):
        loads[2 + c].wait()
        for k in range(0, cols, tile):
            values = _dot(tok[...], vw[c, :, k : k + tile]).astype(BF16).astype(F32)
            weighted = values * _dot(shares, spread[:, c * cols + k : c * cols + k + tile])
            acc = weighted[:rows]
            for v in range(1, n_vars):
                acc = acc + weighted[v * rows : (v + 1) * rows]
            part[c, :, k : k + tile] = acc.astype(BF16)
        if c == 0:
            pl.semaphore_wait(barrier, greeted)
        a_copies.append([])
        for d in far_first(ny):
            peer = lax.rem(y + d, ny)
            theirs = pl.ds(pl.multiple_of(peer * band, band), band)
            if c == 0:
                stat_copies.append(
                    go(stat.at[peer], rstat.at[d], as_send.at[d], as_recv.at[d], at_y(d))
                )
            a_copies[c].append(
                go(part.at[c, theirs], rpart.at[c, d], a_send.at[c, d], a_recv.at[c, d], at_y(d))
            )

    mine = pl.ds(pl.multiple_of(y * band, band), band)
    for copy in stat_copies:
        copy.wait_recv()
    shares, lse = _shares(
        [_unpack(stat[y], heads)] + [_unpack(rstat[d], heads) for d in range(1, ny)]
    )
    zstat[0, :, : 2 * heads] = _pack(lse)
    stat_copy = go(zstat.at[0], zstat.at[1], z_send.at[0], z_recv.at[0], at_zh())
    wide = _widen(shares, spread)
    z_copies = []
    for c in range(CHUNKS):
        for copy in a_copies[c]:
            copy.wait_recv()
        zpart[c, 0] = _weigh(
            [part[c, mine, :]] + [rpart[c, d] for d in range(1, ny)],
            wide[:, c * cols : (c + 1) * cols],
        ).astype(BF16)
        z_copies.append(
            go(zpart.at[c, 0], zpart.at[c, 1], z_send.at[1 + c], z_recv.at[1 + c], at_zh())
        )
    stat_copy.wait_recv()
    shares, _ = _shares([_unpack(zstat[k], heads) for k in range(2)])
    wide = _widen(shares, spread)
    for c in range(CHUNKS):
        z_copies[c].wait_recv()
        cut = slice(c * cols, (c + 1) * cols)
        merged = _weigh([zpart[c, 0], zpart[c, 1]], wide[:, cut])
        pooled[:, cut] = merged.astype(BF16).astype(F32)
    rounded = pooled[...]
    centred = rounded - jnp.mean(rounded, axis=1, keepdims=True)
    spread_sq = jnp.mean(centred * centred, axis=1, keepdims=True)
    gain = gain_ref[...].astype(F32).reshape(1, width)
    nbuf[0] = (centred * lax.rsqrt(spread_sq + 1e-05) * gain).astype(BF16)

    copies = [
        go(nbuf.at[0], nbuf.at[d], n_send.at[d], n_recv.at[d], at_y(d)) for d in far_first(ny)
    ]
    qkvw[3 * HEAD :] = jnp.zeros_like(qkvw[3 * HEAD :])
    for load in loads[2 + CHUNKS :]:
        load.wait()
    for copy in copies:
        copy.wait_recv()
    normed = nbuf[...].reshape(rows, width)

    qkv = _dot(normed, qkvw[...], TRANSPOSED)
    kvbuf[0] = qkv[:, : 2 * HEAD].astype(BF16)
    qbuf[0] = (qkv[:, 2 * HEAD :] * HEAD**-0.5).astype(BF16)
    k_copies = {
        t: go(kvbuf.at[0], kvbuf.at[t], k_send.at[t], k_recv.at[t], at_z(t))
        for t in range(NZ - 1, 0, -1)
    }
    q_copies = [
        go(qbuf.at[0], qbuf.at[d], q_send.at[d], q_recv.at[d], at_i(d)) for d in far_first(ni)
    ]
    hidden = jax.nn.gelu(_dot(normed, up[...]), approximate=True).astype(BF16)
    mlp[...] = _dot(hidden, dw[...])

    group = min(GROUP, ni)
    wide_rows = group * rows
    order = range(ni // group - 1, -1, -1)

    def absorb(first, stop, p):
        kv = kvbuf[first:stop].reshape((stop - first) * rows, 2 * HEAD)
        queries = qbuf[p * group : (p + 1) * group].reshape(wide_rows, 2 * HEAD)
        logits = _dot(kv, queries, TRANSPOSED)
        top = jnp.max(logits, axis=0, keepdims=True)
        if first:
            top = jnp.maximum(top, run_stat[p, :1])
        exps = jnp.exp(logits - top)
        total = jnp.sum(exps, axis=0, keepdims=True)
        out = _dot(kv.T[HEAD:], exps.astype(BF16))
        if first:
            scale = jnp.exp(run_stat[p, :1] - top)
            total = total + scale * run_stat[p, 8:9]
            out = out + scale * run_out[p]
        if stop < NZ:
            run_out[p] = out
            run_stat[p, :8] = jnp.broadcast_to(top, (8, wide_rows))
            run_stat[p, 8:] = jnp.broadcast_to(total, (8, wide_rows))
            return
        out = out / total
        lse = jnp.broadcast_to(top + jnp.log(total), (8, wide_rows))
        for k in range(group):
            obuf[group * p + k] = out[:, k * rows : (k + 1) * rows].astype(BF16)
            ostat[group * p + k] = lse[:, k * rows : (k + 1) * rows]

    for copy in q_copies:
        copy.wait_recv()
    cuts = [0, NZ // 2, NZ * 3 // 4, NZ] if NZ % 4 == 0 else [0, NZ // 2, NZ]
    for first, stop in zip(cuts[:-2], cuts[1:-1]):
        for t in range(max(1, first), stop):
            k_copies[t].wait_recv()
        for p in order:
            absorb(first, stop, p)
    for t in range(cuts[-2], NZ):
        k_copies[t].wait_recv()

    returns = []
    for p in order:
        absorb(cuts[-2], NZ, p)
        for d in range(max(1, p * group), (p + 1) * group):
            owner = at_i(-d)
            returns.append(go(obuf.at[d], robuf.at[d], o_send.at[d], o_recv.at[d], owner))
            returns.append(go(ostat.at[d], rostat.at[d], os_send.at[d], os_recv.at[d], owner))
    for copy in returns:
        copy.wait_recv()
    shares, _ = _shares([ostat[0][:1]] + [rostat[d][:1] for d in range(1, ni)])
    attended = obuf[0].astype(F32) * shares[0]
    for d in range(1, ni):
        attended = attended + robuf[d].astype(F32) * shares[d]

    term = _dot(attended.T.astype(BF16), ow[...]) + mlp[...]
    half = band // NZH
    bands = term.reshape(ny, NZH, half, width)
    for h in range(NZH):
        fbuf[h] = bands[:, h].astype(BF16)
        zsum[h] = bands[0, h]
    f_copies = []
    for stage, h in enumerate((1 - zh, zh)):
        f_copies.append([
            go(fbuf.at[h, d], rf.at[stage, d], f_send.at[stage, d], f_recv.at[stage, d], at_y(-d))
            for d in far_first(ny)
        ])

    def summed(stage, h):
        for copy in f_copies[stage]:
            copy.wait_recv()
        total = zsum[h]
        for d in range(1, ny):
            total = total + rf[stage, d].astype(F32)
        return total

    zsend[...] = summed(0, 1 - zh).astype(BF16)
    last = go(zsend, zrecv, z_send.at[1 + CHUNKS], z_recv.at[1 + CHUNKS], at_zh())
    own = pl.ds(pl.multiple_of(zh * half, half), half)
    mine = summed(1, zh) + pooled[own, :]
    last.wait_recv()
    out_ref[...] = (mine + zrecv[...].astype(F32)).astype(BF16)
    for copy in started:
        copy.wait_send()


def per_device(var_tokens, key_query, value_weight, qkv_weight, out_weight, up_weight, down_weight, norm_gain):
    n_vars, rows, width = var_tokens.shape
    ny = lax.axis_size("var") // NZH
    ni = lax.axis_size("space") // NZ
    band = rows // ny
    hidden = up_weight.shape[1]
    cols = width // CHUNKS
    half = band // NZH
    group = min(GROUP, ni)
    any_spec = pl.BlockSpec(memory_space=pl.ANY)
    vmem_spec = pl.BlockSpec(memory_space=pltpu.VMEM)
    dma = pltpu.SemaphoreType.DMA
    vm = pltpu.VMEM
    return pl.pallas_call(
        functools.partial(kernel, ny, ni, n_vars),
        out_shape=jax.ShapeDtypeStruct((half, width), BF16),
        in_specs=[any_spec] * 7 + [vmem_spec],
        out_specs=vmem_spec,
        scratch_shapes=[
            vm((n_vars * rows, width), BF16), vm(key_query.shape[::-1], BF16), vm((CHUNKS, width, cols), BF16),
            vm((4 * HEAD, width), BF16), vm((HEAD, width), BF16), vm((width, hidden), BF16), vm((hidden, width), BF16),
            vm((CHUNKS, rows, cols), BF16), vm((ny, band // 2, 128), F32),
            vm((CHUNKS, ny, band, cols), BF16), vm((ny, band // 2, 128), F32),
            vm((CHUNKS, 2, band, cols), BF16), vm((2, band // 2, 128), F32),
            vm((band, width), F32), vm((ny, band, width), BF16),
            vm((NZ, rows, 2 * HEAD), BF16), vm((ni, rows, 2 * HEAD), BF16),
            vm((rows, width), F32),
            vm((ni // group, HEAD, group * rows), F32), vm((ni // group, 16, group * rows), F32),
            vm((ni, HEAD, rows), BF16), vm((ni, 8, rows), F32),
            vm((ni, HEAD, rows), BF16), vm((ni, 8, rows), F32),
            vm((NZH, ny, half, width), BF16), vm((NZH, ny, half, width), BF16),
            vm((NZH, half, width), F32), vm((half, width), BF16), vm((half, width), BF16),
            dma((7 + CHUNKS,)), dma((CHUNKS, ny)), dma((CHUNKS, ny)), dma((ny,)), dma((ny,)),
            dma((2 + CHUNKS,)), dma((2 + CHUNKS,)),
            dma((ny,)), dma((ny,)), dma((NZ,)), dma((NZ,)), dma((ni,)), dma((ni,)),
            dma((ni,)), dma((ni,)), dma((ni,)), dma((ni,)), dma((NZH, ny)), dma((NZH, ny)),
        ],
        compiler_params=pltpu.CompilerParams(collective_id=0, has_side_effects=True),
    )(
        var_tokens.reshape(n_vars * rows, width), key_query.T, value_weight,
        qkv_weight.transpose(1, 2, 0).reshape(3 * HEAD, width),
        out_weight, up_weight, down_weight, norm_gain,
    )


def solution(mesh):
    placed = (
        P("var", "space", None), P(), P(), P(None, None, "var"),
        P("var", None), P(None, "var"), P("var", None), P(),
    )
    return jax.shard_map(
        per_device, mesh=mesh, in_specs=placed, out_specs=P(("space", "var"), None), check_vma=False
    )
```
